256 devices in a mesh: seg: 4 (over x), block: 64 (over z, y, core).
Axes of the slice: x: 4, y: 4, z: 8, core: 2. Of those that a mesh axis runs over, the one named last changes fastest.
Arguments:
- jacobian: float32 [1024, 128, 128], P(('seg', 'block')), may hold values from -2 to 2
- implicit_inv: float32 [1024, 128, 128], P(('seg', 'block')), may hold values from -2 to 2, as said below
- input_map: float32 [1024, 128, 64], P(('seg', 'block')), may hold values from -0.75 to 0.75
- controls: float32 [1024, 64], P(('seg', 'block')), may hold values from -2 to 2
- control_step: float32 [1024, 64], P(('seg', 'block')), may hold values from -2 to 2
- state_traj: float32 [1024, 128], P(('seg', 'block')), may hold values from -2 to 2
- terminal: float32 [128], replicated, may hold values from -2 to 2
- init_gap: float32 [128], replicated, may hold values from -3 to 3
- counts: int32 [256], P(('seg', 'block')), may hold values from 2 to 4, as said below
Outputs:
- updated: float32 [1024, 128], P(('seg', 'block'))
- defect_out: float32 [1024, 128], P(('seg', 'block'))
The draws below stay inside these ranges and needn't reach their ends.
Inputs may be any that keep to these rules, and one draw needn't show every extreme that they name: implicit_inv[k] is the inverse of I - jacobian[k] / 2 + jacobian[k] jacobian[k] / 12. `counts`: some block uses all 4 slots and some only half of 4, rounded down; used slots are the first ones of a block.
All inputs are finite; a program needn't handle non-finite values.
Results may differ from the reference program's by a relative error of at most 0.0003.
Values sent between devices are 32-bit elements; how exact they have to be, the bound alone decides.
No kernel may reach another device: no remote copies, remote signals or barrier semaphores. Data moves between devices by JAX's collectives and lax.ppermute only.
A program may use at most 64 MiB of HBM per device.

```python
import math
import jax
import jax.numpy as jnp
from jax import lax

NS = 128
NU = 64
KNOTS_DEV = 4
BLOCKS = 256
KNOTS = 1024


def dynamics_field(key):
    base_key = jax.random.fold_in(key, 71)
    key_skew, key_damping = jax.random.split(base_key)
    entries = jax.random.normal(key_skew, (KNOTS, NS, NS), jnp.float32)
    skew = 0.5 * (entries - jnp.swapaxes(entries, 1, 2)) / math.sqrt(2.0 * NS)
    damping = jnp.exp(jax.random.uniform(key_damping, (KNOTS, NS), jnp.float32, math.log(0.05), math.log(5.0))) / KNOTS
    return skew - damping[:, :, None] * jnp.eye(NS, dtype=jnp.float32)[None]


def draw_jacobian(key, part):
    return dynamics_field(key)


def draw_implicit_inv(key, part):
    field = dynamics_field(key)
    squared = jnp.einsum('kij,kjl->kil', field, field, precision=lax.Precision.HIGHEST)
    implicit = jnp.eye(NS, dtype=jnp.float32)[None] - 0.5 * field + squared / 12.0
    return jnp.linalg.inv(implicit).astype(jnp.float32)


def draw_counts(key, part):
    base_key = jax.random.fold_in(key, 29)
    values = jax.random.randint(base_key, (BLOCKS,), KNOTS_DEV // 2, KNOTS_DEV + 1)
    order = jax.random.permutation(jax.random.fold_in(base_key, 3), BLOCKS)
    values = values.at[order[0]].set(KNOTS_DEV)
    values = values.at[order[1]].set(KNOTS_DEV // 2)
    return values.astype(jnp.int32)


def shard_levels(key, dims, cuts, smallest, largest):
    factor_of = 1.0
    for dim, blocks in cuts:
        draws = jax.random.uniform(jax.random.fold_in(jax.random.fold_in(key, 6), dim), (blocks,), jnp.float32, smallest / len(cuts), largest / len(cuts))
        factor_of = factor_of * jnp.repeat(jnp.exp(draws), dims[dim] // blocks).reshape((-1,) + (1,) * (len(dims) - 1 - dim))
    return factor_of


def noise(stream_key, extent, spread, reach, cuts=(), kind=jnp.bfloat16):
    values = jax.random.normal(stream_key, extent, jnp.float32) * spread
    if len(cuts) > 0:
        values = shard_levels(stream_key, extent, cuts, -0.22, 0.18) * values
    return jnp.clip(values, min=-reach, max=reach).astype(kind)


def setup_inputs(seed: int = 0) -> dict:
    key_list = jax.random.split(jax.random.key(seed), 10)
    return {
        "jacobian": draw_jacobian(jax.random.fold_in(key_list[9], 71), 0),
        "implicit_inv": draw_implicit_inv(jax.random.fold_in(key_list[9], 71), 0),
        "input_map": noise(key_list[2], (KNOTS, NS, NU), NU ** -0.5, 0.75, ((0, 256),), jnp.float32),
        "controls": noise(key_list[3], (KNOTS, NU), 0.25, 2.0, ((0, 256),), jnp.float32),
        "control_step": noise(key_list[4], (KNOTS, NU), 0.25, 2.0, ((0, 256),), jnp.float32),
        "state_traj": noise(key_list[5], (KNOTS, NS), 0.25, 2.0, ((0, 256),), jnp.float32),
        "terminal": noise(key_list[6], (NS,), 0.25, 2.0, (), jnp.float32),
        "init_gap": noise(key_list[7], (NS,), 0.5, 3.0, (), jnp.float32),
        "counts": draw_counts(jax.random.fold_in(key_list[9], 71), 0),
    }


def matvec(matrix, vector):
    return jnp.dot(matrix, vector, precision=lax.Precision.HIGHEST)

def reference(jacobian, implicit_inv, input_map, controls, control_step, state_traj, terminal, init_gap, counts):
    slot_ids = jnp.arange(KNOTS).astype(jnp.int32)
    device_ids = slot_ids // KNOTS_DEV
    within = slot_ids % KNOTS_DEV
    limits = counts[device_ids]
    active = within < limits
    later_ids = jnp.minimum(slot_ids + 1, KNOTS - 1).astype(jnp.int32)
    first_ids = jnp.minimum((device_ids + 1) * KNOTS_DEV, KNOTS - 1).astype(jnp.int32)
    first_state = jnp.where((device_ids + 1 < BLOCKS)[:, None], state_traj[first_ids], terminal[None])
    next_state = jnp.where((within + 1 < limits)[:, None], state_traj[later_ids], first_state)

    def advance(current, pieces):
        dynamics, inverse, input_mat, control, delta_ctrl, present, upcoming, is_active = pieces
        moved = matvec(dynamics, present)
        explicit_x = present + 0.5 * moved + matvec(dynamics, moved) / 12.0
        moved_next = matvec(dynamics, upcoming)
        implicit_x = upcoming - 0.5 * moved_next + matvec(dynamics, moved_next) / 12.0
        defect = implicit_x - explicit_x - matvec(input_mat, control)
        moved_corr = matvec(dynamics, current)
        explicit_c = current + 0.5 * moved_corr + matvec(dynamics, moved_corr) / 12.0
        fresh_state = matvec(inverse, explicit_c + matvec(input_mat, delta_ctrl) - defect)
        carried = jnp.where(is_active, fresh_state, current)
        result = jnp.where(is_active, upcoming + fresh_state, jnp.zeros_like(upcoming))
        defect_kept = jnp.where(is_active, defect, jnp.zeros_like(defect))
        return (carried, (result, defect_kept))
    _, outputs = lax.scan(advance, init_gap.astype(jnp.float32), (jacobian, implicit_inv, input_map, controls, control_step, state_traj, next_state, active))
    return (outputs[0], outputs[1])
```

```python
import functools

import jax
import jax.numpy as jnp
from jax import lax
from jax.experimental import pallas as pl
from jax.experimental.pallas import tpu as pltpu
from jax.sharding import Mesh
from jax.sharding import PartitionSpec as P

AXES = ("seg", "z", "y", "core")
ROWS = 136


NN = (((1,), (0,)), ((), ()))
NT = (((1,), (1,)), ((), ()))


def parts(value, count=2):
    pieces = []
    for _ in range(count):
        piece = value.astype(jnp.bfloat16)
        pieces.append(piece)
        value = value - piece.astype(jnp.float32)
    return pieces


def product(left, right, dims=NN):
    pairs = [(i, j) for i in range(len(left)) for j in range(len(left) - i)]
    pairs = pairs[::-1]
    (left_axis,), (right_axis,) = dims[0]
    return lax.dot_general(
        jnp.concatenate([left[i] for i, _ in pairs], axis=left_axis),
        jnp.concatenate([right[j] for _, j in pairs], axis=right_axis),
        dims,
        preferred_element_type=jnp.float32,
    )


exact = functools.partial(parts, count=3)


def rows_of(shape):
    return lax.broadcasted_iota(jnp.int32, shape, 0)


def eye_of(shape):
    return jnp.where(rows_of(shape) == lax.broadcasted_iota(jnp.int32, shape, 1), 1.0, 0.0)


def compose(earlier, later):
    width = earlier.shape[1]
    out = product(parts(earlier), parts(later[:width]))
    row = rows_of(out.shape)
    return jnp.where(row < width, out, jnp.where(row == width, out + later, earlier))


def maps_kernel(
    counts, jacobian, inverse, input_map, controls, control_step, states, gap, total, partial
):
    knots, width = states.shape
    first = jnp.bool_(True)
    for name in AXES:
        first = jnp.logical_and(first, lax.axis_index(name) == 0)
    start = jnp.where(first, gap[...] + states[0:1, :], 0.0)
    row = rows_of((ROWS, width))
    eye = eye_of((ROWS, width))
    drive = exact(controls[...] + control_step[...])
    running = None
    for k in range(knots):
        pushed = product(drive, exact(input_map[k]))
        left = jnp.concatenate(
            [jacobian[k].T, jnp.broadcast_to(pushed[k : k + 1], (ROWS - width, width))], axis=0
        )
        step = product(exact(left), exact(inverse[k]), NT) + eye
        step = jnp.where(k < counts[0], step, eye)
        matrix = exact(step[:width])
        if k == 0:
            moved = product(exact(jnp.broadcast_to(start, (8, width))), matrix)
            running = step + jnp.where(row >= width, jnp.broadcast_to(moved[0:1], step.shape), 0.0)
        else:
            running = product(exact(running), matrix) + jnp.where(row >= width, step, 0.0)
        partial[k] = running
    total[...] = jnp.where(row == width + 1, jnp.broadcast_to(states[0:1, :], running.shape), running)


def defect_kernel(counts, jacobian, input_map, controls, states, base, last):
    knots, width = states.shape
    count = counts[0]
    slot = rows_of((knots, width))
    here = states[...]
    following = jnp.concatenate([here[1:], jnp.zeros((1, width), jnp.float32)], axis=0)
    following = jnp.where(slot + 1 < count, following, 0.0)
    plus = following + here
    minus = following - here
    both = parts(jnp.concatenate([plus, minus], axis=0))
    forces = parts(controls[...])
    rows = []
    for k in range(knots):
        matrix = parts(jacobian[k])
        once = product(both, matrix, NT)
        twice = product(parts(once), matrix, NT)
        forced = product(forces, parts(input_map[k]))
        rows.append(
            minus[k : k + 1]
            - 0.5 * once[k : k + 1]
            + twice[knots + k : knots + k + 1] / 12.0
            - forced[k : k + 1]
        )
    base[...] = jnp.where(slot < count, jnp.concatenate(rows, axis=0), 0.0)
    last[...] = jacobian[count - 1]


def pair_kernel(axis, own, other, total):
    odd = lax.axis_index(axis) % 2 == 1
    mine, theirs = own[...], other[...]
    total[...] = compose(jnp.where(odd, theirs, mine), jnp.where(odd, mine, theirs))


def choose(pair):
    if pair[0] is pair[1]:
        return pair[0][...]
    return jnp.where(lax.axis_index("core") == 0, pair[0][...], pair[1][...])


def four_kernel(axis, shift, own, *refs):
    near, far, cross = refs[0:2], refs[2:4], refs[4:6]
    total, beside, others = refs[6:]
    place = lax.axis_index(axis) >> shift
    odd = place % 2 == 1
    high = place >= 2
    a, b, c, d = own[...], choose(near), choose(far), choose(cross)
    beside[...] = b
    mine = compose(jnp.where(odd, b, a), jnp.where(odd, a, b))
    rest = compose(jnp.where(odd, d, c), jnp.where(odd, c, d))
    others[...] = rest
    total[...] = compose(jnp.where(high, rest, mine), jnp.where(high, mine, rest))


def before_kernel(levels, *refs):
    out = refs[-1]
    neutral = eye_of(out.shape)
    before = None
    for (axis, bit), ref in zip(levels, refs):
        present = (lax.axis_index(axis) >> bit) % 2 == 1
        chosen = jnp.where(present, ref[...], neutral)
        before = chosen if before is None else compose(chosen, before)
    out[...] = before


def reach_kernel(before, partial, reach):
    width = before.shape[1]
    row = rows_of(before.shape)
    left = parts(before[...])
    for k in range(partial.shape[0]):
        reach[k] = product(left, parts(partial[k, :width])) + jnp.where(row == width, partial[k], 0.0)


def final_kernel(
    counts, near_a, near_b, far_a, far_b, cross, reach, upcoming, base, last, updated, defect
):
    knots, width = base.shape
    near, far = choose((near_a, near_b)), choose((far_a, far_b))
    x = lax.axis_index("seg")
    count = counts[0]
    slot = rows_of((knots, width))
    start = jnp.where(
        x == 3,
        cross[width : width + 1],
        jnp.where(x == 2, far[width : width + 1], jnp.where(x == 1, near[width : width + 1], 0.0)),
    )

    def wide(row):
        return jnp.broadcast_to(row, (8, width))

    second = jnp.where(x == 3, far, cross[...])
    moved = product(parts(wide(start)), parts(second[:width]))[0:1] + second[width : width + 1]
    start = jnp.where(x >= 2, moved, start)
    moved = product(parts(wide(start)), parts(near[:width]))[0:1] + near[width : width + 1]
    start = parts(wide(jnp.where(x == 3, moved, start)))
    for k in range(knots):
        state = product(start, parts(reach[k, :width]))[0:1] + reach[k, width : width + 1]
        updated[k : k + 1] = jnp.where(k < count, state, 0.0)
    settled = jnp.logical_not(
        jnp.logical_and(
            lax.axis_index("z") == lax.axis_size("z") - 1,
            jnp.logical_and(lax.axis_index("y") == 3, lax.axis_index("core") == 1),
        )
    )
    lead = width + 1
    after = jnp.where(x == 1, cross[lead : lead + 1], near[lead : lead + 1])
    after = jnp.where(jnp.logical_or(settled, x == 3), upcoming[...], after)
    matrix = parts(last[...])
    once = product(parts(wide(after)), matrix, NT)
    twice = product(parts(once), matrix, NT)
    met = after - 0.5 * once[0:1] + twice[0:1] / 12.0
    defect[...] = base[...] + jnp.where(slot == count - 1, jnp.broadcast_to(met, slot.shape), 0.0)


def swap(value, axis, partner):
    return lax.ppermute(value, axis, [(i, partner(i)) for i in range(lax.axis_size(axis))])


SMEM = pl.BlockSpec(memory_space=pltpu.SMEM)
VMEM = pl.BlockSpec(memory_space=pltpu.VMEM)


def call(kernel, out, operands, scalars=0, local=True, held=(), flops=0):
    operands = [
        pltpu.with_memory_space_constraint(value, pltpu.VMEM) if k in held else value
        for k, value in enumerate(operands)
    ]
    single = not isinstance(out, list)
    shapes = [out] if single else out
    make = pltpu.VMEM if local else jax.ShapeDtypeStruct
    shapes = tuple(make(shape, jnp.float32) for shape in shapes)
    result = pl.pallas_call(
        kernel,
        out_shape=shapes,
        in_specs=[SMEM] * scalars + [VMEM] * (len(operands) - scalars),
        out_specs=tuple(VMEM for _ in shapes),
        cost_estimate=pl.CostEstimate(flops=flops, bytes_accessed=400_000, transcendentals=0),
    )(*operands)
    return result[0] if single else result


def body(jacobian, inverse, input_map, controls, control_step, states, terminal, gap, counts):
    knots, width = states.shape
    z, _, core = (lax.axis_index(name) for name in AXES[1:])
    square = (ROWS, width)
    input_map = jnp.swapaxes(input_map, 1, 2)
    total, partial = call(
        maps_kernel,
        [square, (knots, *square)],
        (counts, jacobian, inverse, input_map, controls, control_step, states, gap[None]),
        scalars=1,
    )
    base, last = call(
        defect_kernel,
        [(knots, width), (width, width)],
        (counts, jacobian, input_map, controls, states),
        scalars=1,
        held=range(1, 5),
    )

    def lead(pieces):
        return pieces[width + 1 : width + 2]

    def apart(value, axis, partners):
        size = lax.axis_size(axis)
        pairs = [(i * 2 + c, partners[c](i) * 2 + c) for i in range(size) for c in range(2)]
        return lax.ppermute(value, (axis, "core"), pairs)

    def across(value):
        return swap(value, "core", lambda i: i ^ 1)

    levels = [("core", 0)]
    other = across(total)
    earlier = [other]
    upcoming = lead(other)
    settled = core == 0
    total = call(functools.partial(pair_kernel, "core"), square, (total, other), held=(0, 1))

    def gathered(total, axis, masks, shared, first):
        def both():
            return swap(total, axis, lambda i: i ^ shared)

        def each():
            return apart(total, axis, [lambda i, d=d: i ^ d for d in masks])

        if first:
            common, own = both(), each()
        else:
            own, common = each(), both()
        passed = across(own)
        return {shared: (common, common), masks[0]: (own, passed), masks[1]: (passed, own)}

    def one(arrival):
        return jnp.where(core == 0, lead(arrival[0]), lead(arrival[1]))

    def four(total, upcoming, settled, axis, shift, arrivals):
        place = lax.axis_index(axis) >> shift
        operands = [total]
        for arrival in arrivals:
            operands.extend(arrival)
        whole, near, others = call(
            functools.partial(four_kernel, axis, shift), [square, square, square], operands, held=range(7)
        )
        after = jnp.where(place % 2 == 1, one(arrivals[2]), one(arrivals[0]))
        upcoming = jnp.where(settled, upcoming, after)
        settled = jnp.logical_or(settled, place < 3)
        levels.extend([(axis, shift), (axis, shift + 1)])
        earlier.extend([near, others])
        return whole, upcoming, settled

    found = gathered(total, "y", (2, 1), 3, False)
    total, upcoming, settled = four(total, upcoming, settled, "y", 0, [found[1], found[2], found[3]])
    levels.append(("z", 0))
    other = swap(total, "z", lambda i: i ^ 1)
    earlier.append(other)
    upcoming = jnp.where(settled, upcoming, lead(other))
    settled = jnp.logical_or(settled, z % 2 == 0)
    total = call(functools.partial(pair_kernel, "z"), square, (total, other), held=(0, 1))
    found = gathered(total, "z", (6, 5), 2, True)
    total, upcoming, settled = four(total, upcoming, settled, "z", 1, [found[2], found[5], found[6]])
    upcoming = jnp.where(jnp.logical_and(~settled, lax.axis_index("seg") == 3), terminal[None], upcoming)
    found = gathered(total, "seg", (2, 1), 3, False)
    before = call(functools.partial(before_kernel, levels), square, earlier, held=range(len(earlier)))
    reach = call(reach_kernel, (knots, *square), (before, partial), held=(0, 1))
    updated, defect = call(
        final_kernel,
        [(knots, width), (knots, width)],
        (counts, *found[1], *found[2], *found[3][:1], reach, upcoming, base, last),
        scalars=1,
        local=False,
        held=range(1, 10),
    )
    return updated, defect


def solution(mesh):
    split = Mesh(mesh.devices.reshape(mesh.shape["seg"], 8, 4, 2), AXES)
    in_specs = (
        P(AXES, None, None),
        P(AXES, None, None),
        P(AXES, None, None),
        P(AXES, None),
        P(AXES, None),
        P(AXES, None),
        P(),
        P(),
        P(AXES),
    )
    out_specs = (P(AXES, None), P(AXES, None))
    return jax.shard_map(body, mesh=split, in_specs=in_specs, out_specs=out_specs, check_vma=False)
```

```python
import functools

import jax
import jax.numpy as jnp
from jax import lax
from jax.experimental import pallas as pl
from jax.experimental.pallas import tpu as pltpu
from jax.sharding import Mesh
from jax.sharding import PartitionSpec as P

AXES = ("seg", "z", "y", "core")
ROWS = 136


NN = (((1,), (0,)), ((), ()))
NT = (((1,), (1,)), ((), ()))


def parts(value, count=2):
    pieces = []
    for _ in range(count):
        piece = value.astype(jnp.bfloat16)
        pieces.append(piece)
        value = value - piece.astype(jnp.float32)
    return pieces


def product(left, right, dims=NN):
    pairs = [(i, j) for i in range(len(left)) for j in range(len(left) - i)]
    pairs = pairs[::-1]
    (left_axis,), (right_axis,) = dims[0]
    return lax.dot_general(
        jnp.concatenate([left[i] for i, _ in pairs], axis=left_axis),
        jnp.concatenate([right[j] for _, j in pairs], axis=right_axis),
        dims,
        preferred_element_type=jnp.float32,
    )


exact = functools.partial(parts, count=3)


def rows_of(shape):
    return lax.broadcasted_iota(jnp.int32, shape, 0)


def eye_of(shape):
    return jnp.where(rows_of(shape) == lax.broadcasted_iota(jnp.int32, shape, 1), 1.0, 0.0)


def compose(earlier, later):
    width = earlier.shape[1]
    out = product(parts(earlier), parts(later[:width]))
    row = rows_of(out.shape)
    return jnp.where(row < width, out, jnp.where(row == width, out + later, earlier))


def joined(earlier, later):
    out = product(exact(earlier), exact(later[: earlier.shape[1]]))
    return out + jnp.where(rows_of(out.shape) >= earlier.shape[1], later, 0.0)


def maps_kernel(
    counts, jacobian, inverse, input_map, controls, control_step, states, gap, total, *slots
):
    knots, width = states.shape
    first = jnp.bool_(True)
    for name in AXES:
        first = jnp.logical_and(first, lax.axis_index(name) == 0)
    start = jnp.where(first, gap[...] + states[0:1, :], 0.0)
    row = rows_of((ROWS, width))
    eye = eye_of((ROWS, width))
    drive = exact(controls[...] + control_step[...])
    steps = []
    for k in range(knots):
        pushed = product(drive, exact(input_map[k]))[k : k + 1]
        fixed = eye
        if k == 0:
            pushed += product(exact(jnp.broadcast_to(start, (8, width))), exact(jacobian[k]), NT)[0:1]
            fixed = eye + jnp.where(row >= width, jnp.broadcast_to(start, eye.shape), 0.0)
        left = jnp.concatenate(
            [jacobian[k].T, jnp.broadcast_to(pushed, (ROWS - width, width))], axis=0
        )
        step = product(exact(left), exact(inverse[k]), NT) + fixed
        steps.append(step if k < knots // 2 else jnp.where(k < counts[0], step, eye))
    half = joined(steps[0], steps[1])
    whole = joined(half, joined(steps[2], steps[3]))
    for ref, value in zip(slots, (steps[0], half, steps[2], whole)):
        ref[...] = value
    total[...] = jnp.where(row == width + 1, jnp.broadcast_to(states[0:1, :], whole.shape), whole)


def defect_kernel(counts, jacobian, input_map, controls, states, half, step, base, last, third):
    knots, width = states.shape
    count = counts[0]
    slot = rows_of((knots, width))
    here = states[...]
    following = jnp.concatenate([here[1:], jnp.zeros((1, width), jnp.float32)], axis=0)
    following = jnp.where(slot + 1 < count, following, 0.0)
    plus = following + here
    minus = following - here
    both = parts(jnp.concatenate([plus, minus], axis=0))
    forces = parts(controls[...])
    rows = []
    for k in range(knots):
        matrix = parts(jacobian[k])
        once = product(both, matrix, NT)
        twice = product(parts(once), matrix, NT)
        forced = product(forces, parts(input_map[k]))
        rows.append(
            minus[k : k + 1]
            - 0.5 * once[k : k + 1]
            + twice[knots + k : knots + k + 1] / 12.0
            - forced[k : k + 1]
        )
    base[...] = jnp.where(slot < count, jnp.concatenate(rows, axis=0), 0.0)
    last[...] = jacobian[count - 1]
    third[...] = joined(half[...], step[...])


def pair_kernel(axis, own, other, total):
    odd = lax.axis_index(axis) % 2 == 1
    mine, theirs = own[...], other[...]
    total[...] = compose(jnp.where(odd, theirs, mine), jnp.where(odd, mine, theirs))


def arrived(own, passed, common):
    first = lax.axis_index("core") == 0
    return jnp.where(first, own, passed), jnp.where(first, passed, own), common


def four_kernel(axis, shift, ring, own, *refs):
    total, beside, others = refs[-3:]
    place = lax.axis_index(axis) >> shift
    odd = place % 2 == 1
    high = place >= 2
    a = own[...]
    behind, c, ahead = arrived(*(ref[...] for ref in refs[:3]))
    if ring:
        b, d = jnp.where(odd, behind, ahead), jnp.where(odd, ahead, behind)
    else:
        b, d = ahead, behind
    beside[...] = b
    mine = compose(jnp.where(odd, b, a), jnp.where(odd, a, b))
    rest = compose(jnp.where(odd, d, c), jnp.where(odd, c, d))
    others[...] = rest
    total[...] = compose(jnp.where(high, rest, mine), jnp.where(high, mine, rest))


def before_kernel(levels, *refs):
    out = refs[-1]
    neutral = eye_of(out.shape)
    before = None
    for (axis, bit), ref in zip(levels, refs):
        present = (lax.axis_index(axis) >> bit) % 2 == 1
        chosen = jnp.where(present, ref[...], neutral)
        before = chosen if before is None else compose(chosen, before)
    out[...] = before


def reach_kernel(before, *refs):
    reach = refs[-1]
    width = before.shape[1]
    row = rows_of(before.shape)
    left = parts(before[...])
    for k, ref in enumerate(refs[:-1]):
        reach[k] = product(left, parts(ref[:width])) + jnp.where(row == width, ref[...], 0.0)


def final_kernel(counts, reach, upcoming, base, last, own, passed, common, updated, defect):
    knots, width = base.shape
    x = lax.axis_index("seg")
    count = counts[0]
    slot = rows_of((knots, width))
    back, back2, ahead = arrived(own[...], passed[...], common[...])

    def wide(row):
        return jnp.broadcast_to(row, (8, width))

    def moved(start, way):
        return product(parts(wide(start)), parts(way[:width]))[0:1] + way[width : width + 1]

    start = jnp.where(x == 3, ahead, jnp.where(x == 2, back2, back))[width : width + 1]
    start = jnp.where(x == 0, 0.0, start)
    start = jnp.where(x >= 2, moved(start, jnp.where(x == 3, back2, back)), start)
    start = jnp.where(x == 3, moved(start, back), start)
    start = parts(wide(start))
    for k in range(knots):
        state = product(start, parts(reach[k, :width]))[0:1] + reach[k, width : width + 1]
        updated[k : k + 1] = jnp.where(k < count, state, 0.0)
    settled = jnp.logical_not(
        jnp.logical_and(
            lax.axis_index("z") == lax.axis_size("z") - 1,
            jnp.logical_and(lax.axis_index("y") == 3, lax.axis_index("core") == 1),
        )
    )
    after = ahead[width + 1 : width + 2]
    after = jnp.where(jnp.logical_or(settled, x == 3), upcoming[...], after)
    matrix = parts(last[...])
    once = product(parts(wide(after)), matrix, NT)
    twice = product(parts(once), matrix, NT)
    met = after - 0.5 * once[0:1] + twice[0:1] / 12.0
    defect[...] = base[...] + jnp.where(slot == count - 1, jnp.broadcast_to(met, slot.shape), 0.0)


def swap(value, axis, partner):
    return lax.ppermute(value, axis, [(i, partner(i)) for i in range(lax.axis_size(axis))])


SMEM = pl.BlockSpec(memory_space=pltpu.SMEM)
VMEM = pl.BlockSpec(memory_space=pltpu.VMEM)


def call(kernel, out, operands, scalars=0, local=True, held=(), flops=0):
    operands = [
        pltpu.with_memory_space_constraint(value, pltpu.VMEM) if k in held else value
        for k, value in enumerate(operands)
    ]
    single = not isinstance(out, list)
    shapes = [out] if single else out
    make = pltpu.VMEM if local else jax.ShapeDtypeStruct
    shapes = tuple(make(shape, jnp.float32) for shape in shapes)
    result = pl.pallas_call(
        kernel,
        out_shape=shapes,
        in_specs=[SMEM] * scalars + [VMEM] * (len(operands) - scalars),
        out_specs=tuple(VMEM for _ in shapes),
        cost_estimate=pl.CostEstimate(flops=flops, bytes_accessed=400_000, transcendentals=0),
    )(*operands)
    return result[0] if single else result


def body(jacobian, inverse, input_map, controls, control_step, states, terminal, gap, counts):
    knots, width = states.shape
    z, _, core = (lax.axis_index(name) for name in AXES[1:])
    square = (ROWS, width)
    input_map = jnp.swapaxes(input_map, 1, 2)
    total, step, half, third, whole = call(
        maps_kernel,
        [square] * 5,
        (counts, jacobian, inverse, input_map, controls, control_step, states, gap[None]),
        scalars=1,
    )
    base, last, third = call(
        defect_kernel,
        [(knots, width), (width, width), square],
        (counts, jacobian, input_map, controls, states, half, third),
        scalars=1,
        held=range(1, 7),
    )

    def lead(pieces):
        return pieces[width + 1 : width + 2]

    def apart(value, axis, partners):
        size = lax.axis_size(axis)
        pairs = [(i * 2 + c, partners[c](i) * 2 + c) for i in range(size) for c in range(2)]
        return lax.ppermute(value, (axis, "core"), pairs)

    def across(value):
        return swap(value, "core", lambda i: i ^ 1)

    levels = [("core", 0)]
    other = across(total)
    earlier = [other]
    upcoming = lead(other)
    settled = core == 0
    total = call(functools.partial(pair_kernel, "core"), square, (total, other), held=(0, 1))

    def gathered(total, axis, partners, shared, late):
        def both():
            return swap(total, axis, shared)

        common = None if late else both()
        own = apart(total, axis, partners)
        common = both() if late else common
        passed = across(own)
        return own, passed, common

    def four(total, upcoming, settled, axis, shift, ring, found):
        place = lax.axis_index(axis) >> shift
        whole, near, others = call(
            functools.partial(four_kernel, axis, shift, ring),
            [square, square, square],
            [total, *found],
            held=range(4),
        )
        behind, _, ahead = arrived(*map(lead, found))
        after = ahead if ring else jnp.where(place % 2 == 1, behind, ahead)
        upcoming = jnp.where(settled, upcoming, after)
        settled = jnp.logical_or(settled, place < 3)
        levels.extend([(axis, shift), (axis, shift + 1)])
        earlier.extend([near, others])
        return whole, upcoming, settled

    ring = ([lambda i: (i + 1) % 4, lambda i: (i + 2) % 4], lambda i: (i + 3) % 4)
    found = gathered(total, "y", *ring, True)
    total, upcoming, settled = four(total, upcoming, settled, "y", 0, True, found)
    levels.append(("z", 0))
    other = swap(total, "z", lambda i: i ^ 1)
    earlier.append(other)
    upcoming = jnp.where(settled, upcoming, lead(other))
    settled = jnp.logical_or(settled, z % 2 == 0)
    total = call(functools.partial(pair_kernel, "z"), square, (total, other), held=(0, 1))
    found = gathered(total, "z", [lambda i: i ^ 6, lambda i: i ^ 5], lambda i: i ^ 2, False)
    total, upcoming, settled = four(total, upcoming, settled, "z", 1, False, found)
    upcoming = jnp.where(jnp.logical_and(~settled, lax.axis_index("seg") == 3), terminal[None], upcoming)
    found = gathered(total, "seg", [ring[0][0], lambda i: (2, 3, 1, 0)[i]], ring[1], True)
    before = call(
        functools.partial(before_kernel, levels), square, earlier, held=range(len(earlier))
    )
    reach = call(reach_kernel, (knots, *square), (before, step, half, third, whole), held=range(5))
    updated, defect = call(
        final_kernel,
        [(knots, width), (knots, width)],
        (counts, reach, upcoming, base, last, *found),
        scalars=1,
        local=False,
        held=range(1, 8),
    )
    return updated, defect


def solution(mesh):
    split = Mesh(mesh.devices.reshape(mesh.shape["seg"], 8, 4, 2), AXES)
    in_specs = (
        P(AXES, None, None),
        P(AXES, None, None),
        P(AXES, None, None),
        P(AXES, None),
        P(AXES, None),
        P(AXES, None),
        P(),
        P(),
        P(AXES),
    )
    out_specs = (P(AXES, None), P(AXES, None))
    return jax.shard_map(body, mesh=split, in_specs=in_specs, out_specs=out_specs, check_vma=False)
```

```python
import functools

import jax
import jax.numpy as jnp
from jax import lax
from jax.experimental import pallas as pl
from jax.experimental.pallas import tpu as pltpu
from jax.sharding import Mesh
from jax.sharding import PartitionSpec as P

AXES = ("seg", "z", "y", "core")
ROWS = 136


NN = (((1,), (0,)), ((), ()))
NT = (((1,), (1,)), ((), ()))


def parts(value, count=2):
    pieces = []
    for _ in range(count):
        piece = value.astype(jnp.bfloat16)
        pieces.append(piece)
        value = value - piece.astype(jnp.float32)
    return pieces


def product(left, right, dims=NN):
    pairs = [(i, j) for i in range(len(left)) for j in range(len(left) - i)]
    pairs = pairs[::-1]
    (left_axis,), (right_axis,) = dims[0]
    return lax.dot_general(
        jnp.concatenate([left[i] for i, _ in pairs], axis=left_axis),
        jnp.concatenate([right[j] for _, j in pairs], axis=right_axis),
        dims,
        preferred_element_type=jnp.float32,
    )


exact = functools.partial(parts, count=3)


def rows_of(shape):
    return lax.broadcasted_iota(jnp.int32, shape, 0)


def eye_of(shape):
    return jnp.where(rows_of(shape) == lax.broadcasted_iota(jnp.int32, shape, 1), 1.0, 0.0)


def compose(earlier, later):
    width = earlier.shape[1]
    out = product(parts(earlier), parts(later[:width]))
    row = rows_of(out.shape)
    return jnp.where(row < width, out, jnp.where(row == width, out + later, earlier))


def joined(earlier, later):
    out = product(exact(earlier), exact(later[: earlier.shape[1]]))
    return out + jnp.where(rows_of(out.shape) >= earlier.shape[1], later, 0.0)


def maps_kernel(
    counts, jacobian, inverse, input_map, controls, control_step, states, gap, total, *slots
):
    knots, width = states.shape
    first = jnp.bool_(True)
    for name in AXES:
        first = jnp.logical_and(first, lax.axis_index(name) == 0)
    start = jnp.where(first, gap[...] + states[0:1, :], 0.0)
    row = rows_of((ROWS, width))
    eye = eye_of((ROWS, width))
    drive = exact(controls[...] + control_step[...])
    steps = []
    for k in range(knots):
        pushed = product(drive, exact(input_map[k]))[k : k + 1]
        fixed = eye
        if k == 0:
            pushed += product(exact(jnp.broadcast_to(start, (8, width))), exact(jacobian[k]), NT)[0:1]
            fixed = eye + jnp.where(row >= width, jnp.broadcast_to(start, eye.shape), 0.0)
        left = jnp.concatenate(
            [jacobian[k].T, jnp.broadcast_to(pushed, (ROWS - width, width))], axis=0
        )
        step = product(exact(left), exact(inverse[k]), NT) + fixed
        steps.append(step if k < knots // 2 else jnp.where(k < counts[0], step, eye))
    half = joined(steps[0], steps[1])
    whole = joined(half, joined(steps[2], steps[3]))
    for ref, value in zip(slots, (steps[0], half, steps[2], whole)):
        ref[...] = value
    total[...] = jnp.where(row == width + 1, jnp.broadcast_to(states[0:1, :], whole.shape), whole)


def defect_kernel(counts, jacobian, input_map, controls, states, half, step, base, last, third):
    knots, width = states.shape
    count = counts[0]
    slot = rows_of((knots, width))
    here = states[...]
    following = jnp.concatenate([here[1:], jnp.zeros((1, width), jnp.float32)], axis=0)
    following = jnp.where(slot + 1 < count, following, 0.0)
    plus = following + here
    minus = following - here
    both = parts(jnp.concatenate([plus, minus], axis=0))
    forces = parts(controls[...])
    rows = []
    for k in range(knots):
        matrix = parts(jacobian[k])
        once = product(both, matrix, NT)
        twice = product(parts(once), matrix, NT)
        forced = product(forces, parts(input_map[k]))
        rows.append(
            minus[k : k + 1]
            - 0.5 * once[k : k + 1]
            + twice[knots + k : knots + k + 1] / 12.0
            - forced[k : k + 1]
        )
    base[...] = jnp.where(slot < count, jnp.concatenate(rows, axis=0), 0.0)
    last[...] = jacobian[count - 1]
    third[...] = joined(half[...], step[...])


def pair_kernel(axes, own, other, total):
    odd = sum(lax.axis_index(axis) for axis in axes) % 2 == 1
    mine, theirs = own[...], other[...]
    total[...] = compose(jnp.where(odd, theirs, mine), jnp.where(odd, mine, theirs))


def arrived(own, passed, common):
    first = lax.axis_index("core") == 0
    return jnp.where(first, own, passed), jnp.where(first, passed, own), common


def four_kernel(axis, shift, ring, own, *refs):
    total, beside, others = refs[-3:]
    place = lax.axis_index(axis) >> shift
    odd = place % 2 == 1
    high = place >= 2
    a = own[...]
    behind, c, ahead = arrived(*(ref[...] for ref in refs[:3]))
    if ring == 1:
        b, d = jnp.where(odd, behind, ahead), jnp.where(odd, ahead, behind)
    elif ring == 2:
        b, d = behind, ahead
    else:
        b, d = ahead, behind
    beside[...] = b
    mine = compose(jnp.where(odd, b, a), jnp.where(odd, a, b))
    rest = compose(jnp.where(odd, d, c), jnp.where(odd, c, d))
    others[...] = rest
    total[...] = compose(jnp.where(high, rest, mine), jnp.where(high, mine, rest))


def before_kernel(levels, *refs):
    out = refs[-1]
    neutral = eye_of(out.shape)
    before = None
    for (axis, bit), ref in zip(levels, refs):
        present = (lax.axis_index(axis) >> bit) % 2 == 1
        chosen = jnp.where(present, ref[...], neutral)
        before = chosen if before is None else compose(chosen, before)
    out[...] = before


def reach_kernel(before, *refs):
    reach = refs[-1]
    width = before.shape[1]
    row = rows_of(before.shape)
    left = parts(before[...])
    for k, ref in enumerate(refs[:-1]):
        reach[k] = product(left, parts(ref[:width])) + jnp.where(row == width, ref[...], 0.0)


def final_kernel(counts, reach, upcoming, base, last, own, passed, common, updated, defect):
    knots, width = base.shape
    x = lax.axis_index("seg")
    count = counts[0]
    slot = rows_of((knots, width))
    back, back2, ahead = arrived(own[...], passed[...], common[...])

    def wide(row):
        return jnp.broadcast_to(row, (8, width))

    def moved(start, way):
        return product(parts(wide(start)), parts(way[:width]))[0:1] + way[width : width + 1]

    start = jnp.where(x == 3, ahead, jnp.where(x == 2, back2, back))[width : width + 1]
    start = jnp.where(x == 0, 0.0, start)
    start = jnp.where(x >= 2, moved(start, jnp.where(x == 3, back2, back)), start)
    start = jnp.where(x == 3, moved(start, back), start)
    start = parts(wide(start))
    for k in range(knots):
        state = product(start, parts(reach[k, :width]))[0:1] + reach[k, width : width + 1]
        updated[k : k + 1] = jnp.where(k < count, state, 0.0)
    settled = jnp.logical_not(
        jnp.logical_and(
            lax.axis_index("z") == lax.axis_size("z") - 1,
            jnp.logical_and(lax.axis_index("y") == 3, lax.axis_index("core") == 1),
        )
    )
    after = ahead[width + 1 : width + 2]
    after = jnp.where(jnp.logical_or(settled, x == 3), upcoming[...], after)
    matrix = parts(last[...])
    once = product(parts(wide(after)), matrix, NT)
    twice = product(parts(once), matrix, NT)
    met = after - 0.5 * once[0:1] + twice[0:1] / 12.0
    defect[...] = base[...] + jnp.where(slot == count - 1, jnp.broadcast_to(met, slot.shape), 0.0)


def swap(value, axis, partner):
    return lax.ppermute(value, axis, [(i, partner(i)) for i in range(lax.axis_size(axis))])


SMEM = pl.BlockSpec(memory_space=pltpu.SMEM)
VMEM = pl.BlockSpec(memory_space=pltpu.VMEM)


def call(kernel, out, operands, scalars=0, local=True, held=(), flops=0):
    operands = [
        pltpu.with_memory_space_constraint(value, pltpu.VMEM) if k in held else value
        for k, value in enumerate(operands)
    ]
    single = not isinstance(out, list)
    shapes = [out] if single else out
    make = pltpu.VMEM if local else jax.ShapeDtypeStruct
    shapes = tuple(make(shape, jnp.float32) for shape in shapes)
    result = pl.pallas_call(
        kernel,
        out_shape=shapes,
        in_specs=[SMEM] * scalars + [VMEM] * (len(operands) - scalars),
        out_specs=tuple(VMEM for _ in shapes),
        cost_estimate=pl.CostEstimate(flops=flops, bytes_accessed=400_000, transcendentals=0),
    )(*operands)
    return result[0] if single else result


def body(jacobian, inverse, input_map, controls, control_step, states, terminal, gap, counts):
    knots, width = states.shape
    z, _, core = (lax.axis_index(name) for name in AXES[1:])
    square = (ROWS, width)
    input_map = jnp.swapaxes(input_map, 1, 2)
    total, step, half, third, whole = call(
        maps_kernel,
        [square] * 5,
        (counts, jacobian, inverse, input_map, controls, control_step, states, gap[None]),
        scalars=1,
    )
    base, last, third = call(
        defect_kernel,
        [(knots, width), (width, width), square],
        (counts, jacobian, input_map, controls, states, half, third),
        scalars=1,
        held=range(1, 7),
    )

    def lead(pieces):
        return pieces[width + 1 : width + 2]

    def apart(value, axis, partners):
        size = lax.axis_size(axis)
        pairs = [(i * 2 + c, partners[c](i) * 2 + c) for i in range(size) for c in range(2)]
        return lax.ppermute(value, (axis, "core"), pairs)

    def across(value):
        return swap(value, "core", lambda i: i ^ 1)

    def paired(axes, own, other):
        return call(functools.partial(pair_kernel, axes), square, (own, other), held=(0, 1))

    ring = ([lambda i: (i + 1) % 4, lambda i: (i + 2) % 4], lambda i: (i + 3) % 4)

    levels = [("core", 0)]
    other = across(total)
    back = swap(total, "y", lambda i: i ^ 1)
    earlier = [other]
    upcoming = lead(other)
    settled = core == 0
    total = paired(("core",), total, other)

    def gathered(total, axis, partners, back=None, axes=None):
        own = apart(total, axis, partners)
        if axes is None:
            common = swap(total, axis, back)
        else:
            other = across(back)
            common = paired(axes, back, other)
        passed = across(own)
        return own, passed, common

    def four(total, upcoming, settled, axis, shift, ring, found):
        place = lax.axis_index(axis) >> shift
        whole, near, others = call(
            functools.partial(four_kernel, axis, shift, ring),
            [square, square, square],
            [total, *found],
            held=range(4),
        )
        behind, _, ahead = arrived(*map(lead, found))
        after = jnp.where(place % 2 == 1, behind, ahead)
        if ring:
            after = ahead if ring == 1 else jnp.where(place % 2 == 1, ahead, behind)
        upcoming = jnp.where(settled, upcoming, after)
        settled = jnp.logical_or(settled, place < 3)
        levels.extend([(axis, shift), (axis, shift + 1)])
        earlier.extend([near, others])
        return whole, upcoming, settled

    found = gathered(total, "y", [lambda i: i ^ 3, lambda i: i ^ 2], back, ("core",))
    total, upcoming, settled = four(total, upcoming, settled, "y", 0, 0, found)
    levels.append(("z", 0))
    other = swap(total, "z", lambda i: i ^ 1)
    back = apart(total, "z", [lambda i: i ^ 2, lambda i: i ^ 3])
    earlier.append(other)
    upcoming = jnp.where(settled, upcoming, lead(other))
    settled = jnp.logical_or(settled, z % 2 == 0)
    total = paired(("z",), total, other)
    found = gathered(total, "z", [lambda i: i ^ 6, lambda i: i ^ 5], back, ("z", "core"))
    total, upcoming, settled = four(total, upcoming, settled, "z", 1, 0, found)
    upcoming = jnp.where(jnp.logical_and(~settled, lax.axis_index("seg") == 3), terminal[None], upcoming)
    partners = [ring[0][0], lambda i: (2, 3, 1, 0)[i]]
    found = gathered(total, "seg", partners, ring[1])
    before = call(
        functools.partial(before_kernel, levels), square, earlier, held=range(len(earlier))
    )
    reach = call(reach_kernel, (knots, *square), (before, step, half, third, whole), held=range(5))
    updated, defect = call(
        final_kernel,
        [(knots, width), (knots, width)],
        (counts, reach, upcoming, base, last, *found),
        scalars=1,
        local=False,
        held=range(1, 8),
    )
    return updated, defect


def solution(mesh):
    split = Mesh(mesh.devices.reshape(mesh.shape["seg"], 8, 4, 2), AXES)
    in_specs = (
        P(AXES, None, None),
        P(AXES, None, None),
        P(AXES, None, None),
        P(AXES, None),
        P(AXES, None),
        P(AXES, None),
        P(),
        P(),
        P(AXES),
    )
    out_specs = (P(AXES, None), P(AXES, None))
    return jax.shard_map(body, mesh=split, in_specs=in_specs, out_specs=out_specs, check_vma=False)
```

```python
import functools

import jax
import jax.numpy as jnp
from jax import lax
from jax.experimental import pallas as pl
from jax.experimental.pallas import tpu as pltpu
from jax.sharding import Mesh
from jax.sharding import PartitionSpec as P

AXES = ("seg", "z", "y", "core")
ROWS = 136


NN = (((1,), (0,)), ((), ()))
NT = (((1,), (1,)), ((), ()))


def parts(value, count=2):
    pieces = []
    for _ in range(count):
        piece = value.astype(jnp.bfloat16)
        pieces.append(piece)
        value = value - piece.astype(jnp.float32)
    return pieces


def product(left, right, dims=NN):
    pairs = [(i, j) for i in range(len(left)) for j in range(len(left) - i)]
    pairs = pairs[::-1]
    (left_axis,), (right_axis,) = dims[0]
    return lax.dot_general(
        jnp.concatenate([left[i] for i, _ in pairs], axis=left_axis),
        jnp.concatenate([right[j] for _, j in pairs], axis=right_axis),
        dims,
        preferred_element_type=jnp.float32,
    )


exact = functools.partial(parts, count=3)


def rows_of(shape):
    return lax.broadcasted_iota(jnp.int32, shape, 0)


def eye_of(shape):
    return jnp.where(rows_of(shape) == lax.broadcasted_iota(jnp.int32, shape, 1), 1.0, 0.0)


def compose(earlier, later):
    width = earlier.shape[1]
    out = product(parts(earlier), parts(later[:width]))
    row = rows_of(out.shape)
    return jnp.where(row < width, out, jnp.where(row == width, out + later, earlier))


def joined(earlier, later):
    out = product(exact(earlier), exact(later[: earlier.shape[1]]))
    return out + jnp.where(rows_of(out.shape) >= earlier.shape[1], later, 0.0)


def maps_kernel(
    counts, jacobian, inverse, input_map, controls, control_step, states, gap, total, *slots
):
    knots, width = states.shape
    first = jnp.bool_(True)
    for name in AXES:
        first = jnp.logical_and(first, lax.axis_index(name) == 0)
    start = jnp.where(first, gap[...] + states[0:1, :], 0.0)
    row = rows_of((ROWS, width))
    eye = eye_of((ROWS, width))
    drive = exact(controls[...] + control_step[...])
    steps = []
    for k in range(knots):
        pushed = product(drive, exact(input_map[k]))[k : k + 1]
        fixed = eye
        if k == 0:
            pushed += product(exact(jnp.broadcast_to(start, (8, width))), exact(jacobian[k]), NT)[0:1]
            fixed = eye + jnp.where(row >= width, jnp.broadcast_to(start, eye.shape), 0.0)
        left = jnp.concatenate(
            [jacobian[k].T, jnp.broadcast_to(pushed, (ROWS - width, width))], axis=0
        )
        step = product(exact(left), exact(inverse[k]), NT) + fixed
        steps.append(step if k < knots // 2 else jnp.where(k < counts[0], step, eye))
    half = joined(steps[0], steps[1])
    whole = joined(half, joined(steps[2], steps[3]))
    for ref, value in zip(slots, (steps[0], half, steps[2], whole)):
        ref[...] = value
    total[...] = jnp.where(row == width + 1, jnp.broadcast_to(states[0:1, :], whole.shape), whole)


def defect_kernel(counts, jacobian, input_map, controls, states, half, step, base, last, third):
    knots, width = states.shape
    count = counts[0]
    slot = rows_of((knots, width))
    here = states[...]
    following = jnp.concatenate([here[1:], jnp.zeros((1, width), jnp.float32)], axis=0)
    following = jnp.where(slot + 1 < count, following, 0.0)
    plus = following + here
    minus = following - here
    both = parts(jnp.concatenate([plus, minus], axis=0))
    forces = parts(controls[...])
    rows = []
    for k in range(knots):
        matrix = parts(jacobian[k])
        once = product(both, matrix, NT)
        twice = product(parts(once), matrix, NT)
        forced = product(forces, parts(input_map[k]))
        rows.append(
            minus[k : k + 1]
            - 0.5 * once[k : k + 1]
            + twice[knots + k : knots + k + 1] / 12.0
            - forced[k : k + 1]
        )
    base[...] = jnp.where(slot < count, jnp.concatenate(rows, axis=0), 0.0)
    last[...] = jacobian[count - 1]
    third[...] = joined(half[...], step[...])


def pair_kernel(axes, own, other, total):
    odd = sum(lax.axis_index(axis) for axis in axes) % 2 == 1
    mine, theirs = own[...], other[...]
    total[...] = compose(jnp.where(odd, theirs, mine), jnp.where(odd, mine, theirs))


def arrived(own, passed, common):
    first = lax.axis_index("core") == 0
    return jnp.where(first, own, passed), jnp.where(first, passed, own), common


def four_kernel(axis, shift, ring, own, *refs):
    total, beside, others = refs[-3:]
    place = lax.axis_index(axis) >> shift
    odd = place % 2 == 1
    high = place >= 2
    a = own[...]
    behind, c, ahead = arrived(*(ref[...] for ref in refs[:3]))
    if ring == 1:
        b, d = jnp.where(odd, behind, ahead), jnp.where(odd, ahead, behind)
    elif ring == 2:
        b, d = behind, ahead
    else:
        b, d = ahead, behind
    beside[...] = b
    mine = compose(jnp.where(odd, b, a), jnp.where(odd, a, b))
    rest = compose(jnp.where(odd, d, c), jnp.where(odd, c, d))
    others[...] = rest
    total[...] = compose(jnp.where(high, rest, mine), jnp.where(high, mine, rest))


def before_kernel(levels, *refs):
    out = refs[-1]
    neutral = eye_of(out.shape)
    before = None
    for (axis, bit), ref in zip(levels, refs):
        present = (lax.axis_index(axis) >> bit) % 2 == 1
        chosen = jnp.where(present, ref[...], neutral)
        before = chosen if before is None else compose(chosen, before)
    out[...] = before


def reach_kernel(before, *refs):
    reach = refs[-1]
    width = before.shape[1]
    row = rows_of(before.shape)
    left = parts(before[...])
    for k, ref in enumerate(refs[:-1]):
        reach[k] = product(left, parts(ref[:width])) + jnp.where(row == width, ref[...], 0.0)


def final_kernel(counts, reach, upcoming, base, last, own, passed, common, updated, defect):
    knots, width = base.shape
    x = lax.axis_index("seg")
    count = counts[0]
    slot = rows_of((knots, width))
    back, back2, ahead = arrived(own[...], passed[...], common[...])

    def wide(row):
        return jnp.broadcast_to(row, (8, width))

    def moved(start, way):
        return product(parts(wide(start)), parts(way[:width]))[0:1] + way[width : width + 1]

    start = jnp.where(x == 2, back2, back)[width : width + 1]
    start = jnp.where(x == 3, ahead[0:1], start)
    start = jnp.where(x == 0, 0.0, start)
    start = jnp.where(x >= 2, moved(start, jnp.where(x == 3, back2, back)), start)
    start = jnp.where(x == 3, moved(start, back), start)
    start = parts(wide(start))
    for k in range(knots):
        state = product(start, parts(reach[k, :width]))[0:1] + reach[k, width : width + 1]
        updated[k : k + 1] = jnp.where(k < count, state, 0.0)
    settled = jnp.logical_not(
        jnp.logical_and(
            lax.axis_index("z") == lax.axis_size("z") - 1,
            jnp.logical_and(lax.axis_index("y") == 3, lax.axis_index("core") == 1),
        )
    )
    after = ahead[1:2]
    after = jnp.where(jnp.logical_or(settled, x == 3), upcoming[...], after)
    matrix = parts(last[...])
    once = product(parts(wide(after)), matrix, NT)
    twice = product(parts(once), matrix, NT)
    met = after - 0.5 * once[0:1] + twice[0:1] / 12.0
    defect[...] = base[...] + jnp.where(slot == count - 1, jnp.broadcast_to(met, slot.shape), 0.0)


def swap(value, axis, partner):
    return lax.ppermute(value, axis, [(i, partner(i)) for i in range(lax.axis_size(axis))])


SMEM = pl.BlockSpec(memory_space=pltpu.SMEM)
VMEM = pl.BlockSpec(memory_space=pltpu.VMEM)


def call(kernel, out, operands, scalars=0, local=True, held=(), flops=0):
    operands = [
        pltpu.with_memory_space_constraint(value, pltpu.VMEM) if k in held else value
        for k, value in enumerate(operands)
    ]
    single = not isinstance(out, list)
    shapes = [out] if single else out
    make = pltpu.VMEM if local else jax.ShapeDtypeStruct
    shapes = tuple(make(shape, jnp.float32) for shape in shapes)
    result = pl.pallas_call(
        kernel,
        out_shape=shapes,
        in_specs=[SMEM] * scalars + [VMEM] * (len(operands) - scalars),
        out_specs=tuple(VMEM for _ in shapes),
        cost_estimate=pl.CostEstimate(flops=flops, bytes_accessed=400_000, transcendentals=0),
    )(*operands)
    return result[0] if single else result


def body(jacobian, inverse, input_map, controls, control_step, states, terminal, gap, counts):
    knots, width = states.shape
    z, _, core = (lax.axis_index(name) for name in AXES[1:])
    square = (ROWS, width)
    input_map = jnp.swapaxes(input_map, 1, 2)
    total, step, half, third, whole = call(
        maps_kernel,
        [square] * 5,
        (counts, jacobian, inverse, input_map, controls, control_step, states, gap[None]),
        scalars=1,
    )
    base, last, third = call(
        defect_kernel,
        [(knots, width), (width, width), square],
        (counts, jacobian, input_map, controls, states, half, third),
        scalars=1,
        held=range(1, 7),
    )

    def lead(pieces):
        return pieces[width + 1 : width + 2]

    def apart(value, axis, partners):
        size = lax.axis_size(axis)
        pairs = [(i * 2 + c, partners[c](i) * 2 + c) for i in range(size) for c in range(2)]
        return lax.ppermute(value, (axis, "core"), pairs)

    def across(value):
        return swap(value, "core", lambda i: i ^ 1)

    def paired(axes, own, other):
        return call(functools.partial(pair_kernel, axes), square, (own, other), held=(0, 1))

    ring = ([lambda i: (i + 1) % 4, lambda i: (i + 2) % 4], lambda i: (i + 3) % 4)

    levels = [("core", 0)]
    other = across(total)
    back = swap(total, "y", lambda i: i ^ 1)
    earlier = [other]
    upcoming = lead(other)
    settled = core == 0
    total = paired(("core",), total, other)

    def gathered(total, axis, partners, back=None, axes=None):
        own = apart(total, axis, partners)
        if axes is None:
            common = swap(total[width:], axis, back)
        else:
            other = across(back)
            common = paired(axes, back, other)
        passed = across(own)
        return own, passed, common

    def four(total, upcoming, settled, axis, shift, ring, found):
        place = lax.axis_index(axis) >> shift
        whole, near, others = call(
            functools.partial(four_kernel, axis, shift, ring),
            [square, square, square],
            [total, *found],
            held=range(4),
        )
        behind, _, ahead = arrived(*map(lead, found))
        after = jnp.where(place % 2 == 1, behind, ahead)
        if ring:
            after = ahead if ring == 1 else jnp.where(place % 2 == 1, ahead, behind)
        upcoming = jnp.where(settled, upcoming, after)
        settled = jnp.logical_or(settled, place < 3)
        levels.extend([(axis, shift), (axis, shift + 1)])
        earlier.extend([near, others])
        return whole, upcoming, settled

    found = gathered(total, "y", [lambda i: i ^ 3, lambda i: i ^ 2], back, ("core",))
    total, upcoming, settled = four(total, upcoming, settled, "y", 0, 0, found)
    levels.append(("z", 0))
    other = swap(total, "z", lambda i: i ^ 1)
    back = apart(total, "z", [lambda i: i ^ 2, lambda i: i ^ 3])
    earlier.append(other)
    upcoming = jnp.where(settled, upcoming, lead(other))
    settled = jnp.logical_or(settled, z % 2 == 0)
    total = paired(("z",), total, other)
    found = gathered(total, "z", [lambda i: i ^ 6, lambda i: i ^ 5], back, ("z", "core"))
    total, upcoming, settled = four(total, upcoming, settled, "z", 1, 0, found)
    upcoming = jnp.where(jnp.logical_and(~settled, lax.axis_index("seg") == 3), terminal[None], upcoming)
    partners = [ring[0][0], lambda i: (2, 3, 1, 0)[i]]
    found = gathered(total, "seg", partners, ring[1])
    before = call(
        functools.partial(before_kernel, levels), square, earlier, held=range(len(earlier))
    )
    reach = call(reach_kernel, (knots, *square), (before, step, half, third, whole), held=range(5))
    updated, defect = call(
        final_kernel,
        [(knots, width), (knots, width)],
        (counts, reach, upcoming, base, last, *found),
        scalars=1,
        local=False,
        held=range(1, 8),
    )
    return updated, defect


def solution(mesh):
    split = Mesh(mesh.devices.reshape(mesh.shape["seg"], 8, 4, 2), AXES)
    in_specs = (
        P(AXES, None, None),
        P(AXES, None, None),
        P(AXES, None, None),
        P(AXES, None),
        P(AXES, None),
        P(AXES, None),
        P(),
        P(),
        P(AXES),
    )
    out_specs = (P(AXES, None), P(AXES, None))
    return jax.shard_map(body, mesh=split, in_specs=in_specs, out_specs=out_specs, check_vma=False)
```
